32 devices in a mesh: dp: 16 (over z, x, core), tensor: 2 (over y).
Axes of the slice: x: 2, y: 2, z: 4, core: 2. Of those that a mesh axis runs over, the one named last changes fastest.
Arguments:
- block_in: bfloat16 [16384, 1024], P('dp', 'tensor'), may hold values from -6 to 6
- segment_ids: int32 [32, 512], P('dp'), may hold values from 0 to 7, never falling along the last dimension, each value on 1 to 256 neighbouring positions
- ln1_gain: float32 [1024], P('tensor'), may hold values from 0.1 to 1.9
- ln1_bias: float32 [1024], P('tensor'), may hold values from -4 to 4
- w_qkv: bfloat16 [3, 1024, 1024], P(None, None, 'tensor'), may hold values from -0.1875 to 0.1875
- qv_bias: float32 [2, 1024], P(None, 'tensor'), may hold values from -4 to 4
- w_out: bfloat16 [1024, 1024], P('tensor'), may hold values from -0.75 to 0.75
- out_bias: float32 [1024], P('tensor'), may hold values from -4 to 4
- ln2_gain: float32 [1024], P('tensor'), may hold values from 0.1 to 1.9
- ln2_bias: float32 [1024], P('tensor'), may hold values from -4 to 4
- w_up: bfloat16 [1024, 4096], P(None, 'tensor'), may hold values from -0.1875 to 0.1875
- up_bias: float32 [4096], P('tensor'), may hold values from -4 to 4
- w_down: bfloat16 [4096, 1024], P('tensor'), may hold values from -0.09375 to 0.09375
- down_bias: float32 [1024], P('tensor'), may hold values from -4 to 4
- cotangent: bfloat16 [16384, 1024], P('dp', 'tensor'), may hold values from -6 to 6
Outputs:
- block_out: bfloat16 [16384, 1024], P('dp', 'tensor')
- input_grad: float32 [16384, 1024], P('dp', 'tensor')
- grad_ln1_gain: float32 [1024], P('tensor')
- grad_ln1_bias: float32 [1024], P('tensor')
- grad_qkv: float32 [3, 1024, 1024], P(None, None, 'tensor')
- grad_qv_bias: float32 [2, 1024], P(None, 'tensor')
- grad_out: float32 [1024, 1024], P('tensor')
- grad_out_bias: float32 [1024], P('tensor')
- grad_ln2_gain: float32 [1024], P('tensor')
- grad_ln2_bias: float32 [1024], P('tensor')
- grad_up: float32 [1024, 4096], P(None, 'tensor')
- grad_up_bias: float32 [4096], P('tensor')
- grad_down: float32 [4096, 1024], P('tensor')
- grad_down_bias: float32 [1024], P('tensor')
The draws below stay inside these ranges and needn't reach their ends.
Inputs may be any that keep to these rules, and one draw needn't show every extreme that they name: `segment_ids`: along each packed row of 512 tokens the ids never fall; each id covers 1 to 256 consecutive tokens, one of them exactly 256.
All inputs are finite; a program needn't handle non-finite values.
Results may differ from the reference program's by a relative error of at most 0.0095.
The reference program's roundings to bfloat16 on the way count: a program that leaves them out, or rounds other values in their place, can miss the bound.
Values may be sent and summed in bfloat16 or wider, within the bound.
No kernel may reach another device: no remote copies, remote signals or barrier semaphores. Data moves between devices by JAX's collectives and lax.ppermute only.
A program may use at most 192 MiB of HBM per device.

```python
import math
import jax
import jax.numpy as jnp
import numpy as np
from jax import lax

D = 1024
HEADS = 16
HEAD_DIM = 64
FF = 4096
SEQ = 512
NROWS = 32
TOKENS = 16384


def level_of(key, dims, shards, low, high):
    def one(axis_at, blocks):
        steps = jax.random.uniform(jax.random.fold_in(jax.random.fold_in(key, 6), axis_at), (blocks,), jnp.float32, low / len(shards), high / len(shards))
        return jnp.repeat(jnp.exp(steps), dims[axis_at] // blocks).reshape((-1,) + (1,) * (len(dims) - axis_at - 1))

    loudness = one(*shards[0])
    for cut in shards[1:]:
        loudness = loudness * one(*cut)
    return loudness


def length_profile(amount, total, most, skew):
    portions = [(1 << 20) // math.isqrt(rank ** skew) + 1 for rank in range(2, amount + 1)]
    rest, given = total - most - (amount - 1), [1] * (amount - 1)
    while rest > 0:
        candidates = [i for i in range(amount - 1) if given[i] < most]
        mass, budget = sum([portions[i] for i in candidates]), rest
        for i in candidates:
            addition = min(most - given[i], max(1, budget * portions[i] // mass), rest)
            given[i] = given[i] + addition
            rest = rest - addition
    return np.array([most] + given)


def ragged_sizes(rng, count, total, bound, lean):
    if count == 2:
        one = jax.random.randint(rng, (), max(1, total - bound), min(bound, total - 1) + 1)
        return jnp.stack([one, total - one])
    sizes = jnp.asarray(length_profile(count, total, bound, lean), jnp.int32)
    couples = (count - 1) // 2
    donor, receiver = sizes[1:1 + 2 * couples:2], sizes[2:2 + 2 * couples:2]
    margin = jnp.minimum(donor - 1, bound - receiver)
    shifted = jax.random.randint(jax.random.fold_in(rng, 1), (couples,), 0, 1 << 20) % (margin + 1)
    sizes = sizes.at[1:1 + 2 * couples:2].set(donor - shifted).at[2:2 + 2 * couples:2].set(receiver + shifted)
    return sizes[jax.random.permutation(jax.random.fold_in(rng, 2), count)]


def bell_draw(own_key, dims, spread, most, pieces=(), kind=jnp.bfloat16):
    loudness = level_of(own_key, dims, pieces, -0.22, 0.18) if pieces else 1.0
    array = jax.random.normal(own_key, dims, jnp.float32) * spread * loudness
    return jnp.minimum(jnp.maximum(array, -most), most).astype(kind)


def setup_inputs(seed: int = 0) -> dict:
    arg_keys = jax.random.split(jax.random.key(seed), 16)
    block_in = bell_draw(arg_keys[0], (TOKENS, D), 1.0, 6.0, ((0, 16), (1, 2)))
    segment_ids = jax.vmap(lambda own: jnp.searchsorted(jnp.cumsum(ragged_sizes(own, 8, SEQ, SEQ // 2, 2)), jnp.arange(SEQ), side="right"))(jax.random.split(arg_keys[1], NROWS)).reshape((NROWS, SEQ)).astype(jnp.int32)
    ln1_gain = jnp.clip(1.0 + 0.18 * jax.random.normal(arg_keys[2], (D,), jnp.float32), 0.1, 1.9)
    ln1_bias = bell_draw(arg_keys[3], (D,), 1.0, 4.0, ((0, 2),), jnp.float32)
    w_qkv = bell_draw(arg_keys[4], (3, D, D), D ** -0.5, 0.1875, ((2, 2),))
    qv_bias = bell_draw(arg_keys[5], (2, D), 1.0, 4.0, ((1, 2),), jnp.float32)
    w_out = bell_draw(arg_keys[6], (D, D), (D // 16) ** -0.5, 0.75, ((0, 2),))
    out_bias = bell_draw(arg_keys[7], (D,), 1.0, 4.0, ((0, 2),), jnp.float32)
    ln2_gain = jnp.clip(1.0 + 0.18 * jax.random.normal(arg_keys[8], (D,), jnp.float32), 0.1, 1.9)
    ln2_bias = bell_draw(arg_keys[9], (D,), 1.0, 4.0, ((0, 2),), jnp.float32)
    w_up = bell_draw(arg_keys[10], (D, FF), D ** -0.5, 0.1875, ((1, 2),))
    up_bias = bell_draw(arg_keys[11], (FF,), 1.0, 4.0, ((0, 2),), jnp.float32)
    w_down = bell_draw(arg_keys[12], (FF, D), FF ** -0.5, 0.09375, ((0, 2),))
    down_bias = bell_draw(arg_keys[13], (D,), 1.0, 4.0, ((0, 2),), jnp.float32)
    cotangent = bell_draw(arg_keys[14], (TOKENS, D), 1.0, 6.0, ((0, 16), (1, 2)))
    return dict(block_in=block_in, segment_ids=segment_ids, ln1_gain=ln1_gain, ln1_bias=ln1_bias, w_qkv=w_qkv, qv_bias=qv_bias, w_out=w_out, out_bias=out_bias, ln2_gain=ln2_gain, ln2_bias=ln2_bias, w_up=w_up, up_bias=up_bias, w_down=w_down, down_bias=down_bias, cotangent=cotangent)


norm_eps = 1e-05
gelu_scale = 0.7978845608028654
gelu_cubic = 0.044715

def rounded(value):
    return lax.optimization_barrier(value.astype(jnp.bfloat16))

def gelu_pair(pre_act):
    inner = gelu_scale * (pre_act + gelu_cubic * pre_act * pre_act * pre_act)
    tangent = jnp.tanh(inner)
    value = 0.5 * pre_act * (1.0 + tangent)
    slope = 0.5 * (1.0 + tangent) + 0.5 * pre_act * (1.0 - tangent * tangent) * gelu_scale * (1.0 + 3.0 * gelu_cubic * pre_act * pre_act)
    return (value, slope)

def layer_norm(inputs, gain, shift):
    row_mean = lax.optimization_barrier(jnp.mean(inputs, -1, keepdims=True))
    row_var = lax.optimization_barrier(jnp.mean(inputs * inputs, -1, keepdims=True)) - row_mean * row_mean
    inv_std = lax.rsqrt(row_var + norm_eps)
    centred = (inputs - row_mean) * inv_std
    return (centred * gain + shift, centred, inv_std)

def norm_back(upstream, centred, inv_std, gain):
    scaled = upstream * gain
    return inv_std * (scaled - lax.optimization_barrier(jnp.mean(scaled, -1, keepdims=True)) - centred * lax.optimization_barrier(jnp.mean(scaled * centred, -1, keepdims=True)))

def alibi_terms(segment_rows, slopes):
    length = segment_rows.shape[1]
    position = jnp.arange(length)
    offset = (position[None, :] - position[:, None]).astype(jnp.float32)
    bias_table = slopes[:, None, None] * offset[None]
    allowed = (segment_rows[:, :, None] == segment_rows[:, None, :]) & (position[None, :] <= position[:, None])[None]
    return (bias_table, allowed)

def score_table(query, keys, bias_table, allowed):
    scores = jnp.einsum('rqhc,rkhc->rhqk', query.astype(jnp.float32), keys.astype(jnp.float32)) * HEAD_DIM ** (-0.5) + bias_table[None]
    return jnp.where(allowed[:, None], scores, -jnp.inf)

def attend(query, keys, values, bias_table, allowed):
    scores = score_table(query, keys, bias_table, allowed)
    top_score = lax.optimization_barrier(jnp.max(scores, -1, keepdims=True))
    log_total = top_score + jnp.log(lax.optimization_barrier(jnp.sum(jnp.exp(scores - top_score), -1, keepdims=True)))
    soft_weights = rounded(jnp.exp(scores - log_total))
    context = rounded(jnp.einsum('rhqk,rkhc->rqhc', soft_weights.astype(jnp.float32), values.astype(jnp.float32)))
    return (context, log_total)

def attend_back(query, keys, values, context, log_total, d_context, bias_table, allowed):
    scores = score_table(query, keys, bias_table, allowed)
    probs = jnp.exp(scores - log_total)
    soft_weights = rounded(probs).astype(jnp.float32)
    grad_ctx = d_context.astype(jnp.float32)
    d_probs = jnp.einsum('rqhc,rkhc->rhqk', grad_ctx, values.astype(jnp.float32))
    delta = jnp.einsum('rqhc,rqhc->rhq', grad_ctx, context.astype(jnp.float32))
    d_scores = probs * (d_probs - delta[..., None])
    score_grad = rounded(d_scores).astype(jnp.float32)
    grad_value = jnp.einsum('rhqk,rqhc->rkhc', soft_weights, grad_ctx)
    grad_query = jnp.einsum('rhqk,rkhc->rqhc', score_grad, keys.astype(jnp.float32)) * HEAD_DIM ** (-0.5)
    grad_key = jnp.einsum('rhqk,rqhc->rkhc', score_grad, query.astype(jnp.float32)) * HEAD_DIM ** (-0.5)
    return (grad_query, grad_key, grad_value)

def one_row(x_row, seg_row, g_row, slopes, ln1_gain, ln1_bias, w_qkv, qv_bias, w_out, out_bias, ln2_gain, ln2_bias, w_up, up_bias, w_down, down_bias):
    inputs = x_row.astype(jnp.float32)
    norm1, centred1, inv1 = layer_norm(inputs, ln1_gain, ln1_bias)
    normed1 = rounded(norm1)
    projected = jnp.einsum('td,jde->jte', normed1.astype(jnp.float32), w_qkv.astype(jnp.float32))
    head_shape = (1, SEQ, HEADS, HEAD_DIM)
    query = rounded(projected[0] + qv_bias[0]).reshape(head_shape)
    keys = rounded(projected[1]).reshape(head_shape)
    values = rounded(projected[2] + qv_bias[1]).reshape(head_shape)
    bias_table, allowed = alibi_terms(seg_row[None], slopes)
    context, log_total = attend(query, keys, values, bias_table, allowed)
    context_flat = context.reshape(SEQ, D)
    resid = inputs + jnp.dot(context_flat, w_out, preferred_element_type=jnp.float32) + out_bias
    norm2, centred2, inv2 = layer_norm(resid, ln2_gain, ln2_bias)
    normed2 = rounded(norm2)
    pre_act = jnp.dot(normed2, w_up, preferred_element_type=jnp.float32) + up_bias
    act_value, act_slope = gelu_pair(pre_act)
    act_b = rounded(act_value)
    out_row = (resid + jnp.dot(act_b, w_down, preferred_element_type=jnp.float32) + down_bias).astype(jnp.bfloat16)
    upstream = g_row.astype(jnp.float32)
    grad_down = jnp.dot(act_b.T, g_row, preferred_element_type=jnp.float32)
    grad_down_bias = lax.optimization_barrier(jnp.sum(upstream, 0))
    d_pre = jnp.dot(g_row, w_down.T, preferred_element_type=jnp.float32) * act_slope
    d_pre_b = rounded(d_pre)
    grad_up = jnp.dot(normed2.T, d_pre_b, preferred_element_type=jnp.float32)
    grad_up_bias = lax.optimization_barrier(jnp.sum(d_pre, 0))
    d_norm2 = jnp.dot(d_pre_b, w_up.T, preferred_element_type=jnp.float32)
    grad_ln2_gain = lax.optimization_barrier(jnp.sum(d_norm2 * centred2, 0))
    grad_ln2_bias = lax.optimization_barrier(jnp.sum(d_norm2, 0))
    d_resid = upstream + norm_back(d_norm2, centred2, inv2, ln2_gain)
    d_resid_b = rounded(d_resid)
    grad_out = jnp.dot(context_flat.T, d_resid_b, preferred_element_type=jnp.float32)
    grad_out_bias = lax.optimization_barrier(jnp.sum(d_resid, 0))
    d_context = rounded(jnp.dot(d_resid_b, w_out.T, preferred_element_type=jnp.float32)).reshape(head_shape)
    grad_query, grad_key, grad_value = attend_back(query, keys, values, context, log_total, d_context, bias_table, allowed)
    grad_query = grad_query.reshape(SEQ, D)
    grad_key = grad_key.reshape(SEQ, D)
    grad_value = grad_value.reshape(SEQ, D)
    grad_qv_bias = jnp.stack([lax.optimization_barrier(jnp.sum(grad_query, 0)), lax.optimization_barrier(jnp.sum(grad_value, 0))])
    d_proj = rounded(jnp.stack([grad_query, grad_key, grad_value])).astype(jnp.float32)
    grad_qkv = jnp.einsum('td,jte->jde', normed1.astype(jnp.float32), d_proj)
    d_norm1 = jnp.einsum('jte,jde->td', d_proj, w_qkv.astype(jnp.float32))
    grad_ln1_gain = lax.optimization_barrier(jnp.sum(d_norm1 * centred1, 0))
    grad_ln1_bias = lax.optimization_barrier(jnp.sum(d_norm1, 0))
    grad_input = d_resid + norm_back(d_norm1, centred1, inv1, ln1_gain)
    grads = (grad_ln1_gain, grad_ln1_bias, grad_qkv, grad_qv_bias, grad_out, grad_out_bias, grad_ln2_gain, grad_ln2_bias, grad_up, grad_up_bias, grad_down, grad_down_bias)
    return (out_row, grad_input, grads)

def reference(block_in, segment_ids, ln1_gain, ln1_bias, w_qkv, qv_bias, w_out, out_bias, ln2_gain, ln2_bias, w_up, up_bias, w_down, down_bias, cotangent):
    slopes = jnp.exp2(-8.0 * (jnp.arange(HEADS) + 1).astype(jnp.float32) / HEADS)
    row_inputs = block_in.reshape(NROWS, SEQ, D)
    row_grads = cotangent.reshape(NROWS, SEQ, D)
    params = (ln1_gain, ln1_bias, w_qkv, qv_bias, w_out, out_bias, ln2_gain, ln2_bias, w_up, up_bias, w_down, down_bias)
    initial = (jnp.zeros((D,), jnp.float32), jnp.zeros((D,), jnp.float32), jnp.zeros((3, D, D), jnp.float32), jnp.zeros((2, D), jnp.float32), jnp.zeros((D, D), jnp.float32), jnp.zeros((D,), jnp.float32), jnp.zeros((D,), jnp.float32), jnp.zeros((D,), jnp.float32), jnp.zeros((D, FF), jnp.float32), jnp.zeros((FF,), jnp.float32), jnp.zeros((FF, D), jnp.float32), jnp.zeros((D,), jnp.float32))

    def step(carry, inputs):
        x_row, seg_row, g_row = inputs
        out_row, grad_input, grads = one_row(x_row, seg_row, g_row, slopes, *params)
        return (tuple((total + part for total, part in zip(carry, grads))), (out_row, grad_input))
    totals, (out_rows, input_rows) = lax.scan(step, initial, (row_inputs, segment_ids, row_grads))
    return (out_rows.reshape(TOKENS, D), input_rows.reshape(TOKENS, D), totals[0], totals[1], totals[2], totals[3], totals[4], totals[5], totals[6], totals[7], totals[8], totals[9], totals[10], totals[11])
```

```python
import functools

import jax
import jax.numpy as jnp
from jax import lax
from jax.experimental import pallas as pl
from jax.experimental.pallas import tpu as pltpu
from jax.sharding import PartitionSpec as P

D = 1024
HEADS = 16
HEAD_DIM = 64

norm_eps = 1e-05
gelu_scale = 0.7978845608028654
gelu_cubic = 0.044715
LANES = 128
QB = 256
MASKED = -1e30

f32, bf16 = jnp.float32, jnp.bfloat16


def dims(a, b):
    return (((a,), (b,)), ((), ()))


def mm(a, b, ca, cb):
    return lax.dot_general(a, b, dims(ca, cb), preferred_element_type=f32)


def fill_mask(mask_ref, seg_row, seg_col):
    length = mask_ref.shape[0]
    key = lax.broadcasted_iota(jnp.int32, (length, length), 0)
    qry = lax.broadcasted_iota(jnp.int32, (length, length), 1)
    allowed = (seg_col[0] == seg_row[0]) & (key <= qry)
    mask_ref[...] = jnp.where(allowed, (key - qry).astype(f32), MASKED)


def attend_kernel(slopes, seg_row, seg_col, q_ref, k_ref, v_ref, ctx_ref, lse_ref, mask_ref):
    pair = pl.program_id(1)

    @pl.when(pair == 0)
    def _():
        fill_mask(mask_ref, seg_row, seg_col)

    length = mask_ref.shape[0]
    lane = lax.broadcasted_iota(jnp.int32, (length, LANES), 1)
    sub = lax.broadcasted_iota(jnp.int32, (LANES, QB), 0)
    query = q_ref[0] * HEAD_DIM ** (-0.5)
    keys = k_ref[0]
    values = v_ref[0]
    heads_keys = [jnp.where((lane < HEAD_DIM) == (h == 0), keys, 0.0).astype(bf16) for h in (0, 1)]
    for begin in range(0, length, QB):
        stop = begin + QB
        parts = []
        for h in (0, 1):
            scores = mm(heads_keys[h][:stop], query[begin:stop], 1, 1)
            scores = scores + slopes[2 * pair + h] * mask_ref[:stop, begin:stop]
            top = jnp.max(scores, 0, keepdims=True)
            expo = jnp.exp(scores - top)
            total = jnp.sum(expo, 0, keepdims=True)
            lse_ref[0, 0, h : h + 1, begin:stop] = top + jnp.log(total)
            soft = (expo * (1.0 / total)).astype(bf16)
            parts.append(mm(values[:stop], soft, 0, 0))
        both = jnp.where(sub < HEAD_DIM, parts[0], parts[1])
        ctx_ref[begin:stop, :] = both.T.astype(bf16)


def attend_back_kernel(
    slopes, seg_row, seg_col, q_ref, k_ref, v_ref, ctx_ref, dctx_ref, lse_ref, out_ref, sums_ref, mask_ref
):
    pair = pl.program_id(1)

    @pl.when(pair == 0)
    def _():
        fill_mask(mask_ref, seg_row, seg_col)

    length = mask_ref.shape[0]
    scale = HEAD_DIM ** (-0.5)
    lane = lax.broadcasted_iota(jnp.int32, (length, LANES), 1)
    sub = lax.broadcasted_iota(jnp.int32, (LANES, QB), 0)
    query = q_ref[0] * scale
    keys = k_ref[0]
    values = v_ref[0]
    ctx = ctx_ref[...].astype(f32)
    dctx = dctx_ref[...]
    first = lane < HEAD_DIM
    heads_keys = [jnp.where(first == (h == 0), keys, 0.0).astype(bf16) for h in (0, 1)]
    heads_values = [jnp.where(first == (h == 0), values, 0.0).astype(bf16) for h in (0, 1)]
    grad_k = None
    grad_v = None
    sum_q = jnp.zeros((1, LANES), f32)
    for begin in range(0, length, QB):
        stop = begin + QB
        dctx_b = dctx[begin:stop]
        prod = (dctx_b.astype(f32) * ctx[begin:stop]).T
        gq, gk, gv = [], [], []
        for h in (0, 1):
            delta = jnp.sum(prod[h * HEAD_DIM : (h + 1) * HEAD_DIM], 0, keepdims=True)
            scores = mm(heads_keys[h][:stop], query[begin:stop], 1, 1)
            scores = scores + slopes[2 * pair + h] * mask_ref[:stop, begin:stop]
            probs = jnp.exp(scores - lse_ref[0, 0, h : h + 1, begin:stop])
            soft = probs.astype(bf16)
            d_probs = mm(heads_values[h][:stop], dctx_b, 1, 1)
            d_scores = (probs * (d_probs - delta)).astype(bf16)
            gv.append(mm(soft, dctx_b, 1, 0))
            gk.append(mm(d_scores, query[begin:stop], 1, 0))
            gq.append(mm(keys[:stop], d_scores, 0, 0))
        gq = jnp.where(sub < HEAD_DIM, gq[0], gq[1]).T * scale
        sum_q = sum_q + jnp.sum(gq, 0, keepdims=True)
        out_ref[0, begin:stop, :] = gq.astype(bf16)
        gk = jnp.where(first[:stop], gk[0], gk[1])
        gv = jnp.where(first[:stop], gv[0], gv[1])
        if grad_k is not None:
            gk = jnp.concatenate([gk[:begin] + grad_k, gk[begin:]], 0)
            gv = jnp.concatenate([gv[:begin] + grad_v, gv[begin:]], 0)
        grad_k, grad_v = gk, gv
    out_ref[1, :, :] = grad_k.astype(bf16)
    out_ref[2, :, :] = grad_v.astype(bf16)
    sums_ref[0, 0:1, :] = sum_q
    sums_ref[0, 1:2, :] = jnp.sum(grad_v, 0, keepdims=True)


def attention_specs(length):
    smem = pl.BlockSpec(memory_space=pltpu.SMEM)
    seg_row = pl.BlockSpec((1, 1, length), lambda r, p: (r, 0, 0))
    seg_col = pl.BlockSpec((1, length, 1), lambda r, p: (r, 0, 0))
    qkv = [pl.BlockSpec((1, length, LANES), lambda r, p, j=j: (j, r, p)) for j in range(3)]
    flat = pl.BlockSpec((length, LANES), lambda r, p: (r, p))
    lse = pl.BlockSpec((1, 1, 2, length), lambda r, p: (r, p, 0, 0))
    return smem, seg_row, seg_col, qkv, flat, lse


def attend(projected, seg, slopes):
    rows, length = seg.shape
    tokens, cols = projected.shape[1:]
    pairs = cols // LANES
    smem, seg_row, seg_col, qkv, flat, lse = attention_specs(length)
    return pl.pallas_call(
        attend_kernel,
        grid=(rows, pairs),
        in_specs=[smem, seg_row, seg_col, *qkv],
        out_specs=[flat, lse],
        out_shape=[
            jax.ShapeDtypeStruct((tokens, cols), bf16),
            jax.ShapeDtypeStruct((rows, pairs, 2, length), f32),
        ],
        scratch_shapes=[pltpu.VMEM((length, length), f32)],
        cost_estimate=pl.CostEstimate(
            flops=3 * rows * pairs * 2 * length * length * LANES,
            bytes_accessed=10 * tokens * cols,
            transcendentals=rows * pairs * 2 * length * length,
        ),
        name="attend",
    )(slopes, seg[:, None, :], seg[:, :, None], projected, projected, projected)


def attend_back(projected, context, d_context, lse_in, seg, slopes):
    rows, length = seg.shape
    tokens, cols = context.shape
    pairs = cols // LANES
    smem, seg_row, seg_col, qkv, flat, lse = attention_specs(length)
    return pl.pallas_call(
        attend_back_kernel,
        grid=(rows, pairs),
        in_specs=[smem, seg_row, seg_col, *qkv, flat, flat, lse],
        out_specs=[
            pl.BlockSpec((3, length, LANES), lambda r, p: (0, r, p)),
            pl.BlockSpec((1, 2, LANES), lambda r, p: (r, 0, p)),
        ],
        out_shape=[
            jax.ShapeDtypeStruct((3, tokens, cols), bf16),
            jax.ShapeDtypeStruct((rows, 2, cols), f32),
        ],
        scratch_shapes=[pltpu.VMEM((length, length), f32)],
        cost_estimate=pl.CostEstimate(
            flops=8 * rows * pairs * 2 * length * length * LANES,
            bytes_accessed=16 * tokens * cols,
            transcendentals=rows * pairs * 2 * length * length,
        ),
        name="attend_back",
    )(slopes, seg[:, None, :], seg[:, :, None], projected, projected, projected, context, d_context, lse_in)


def gelu_pair(pre_act):
    square = pre_act * pre_act
    tangent = jnp.tanh(gelu_scale * (pre_act + gelu_cubic * square * pre_act))
    half = 0.5 * (1.0 + tangent)
    slope = half + 0.5 * pre_act * (1.0 - tangent * tangent) * (gelu_scale * (1.0 + 3.0 * gelu_cubic * square))
    return (pre_act * half, slope)


def feed_kernel(first, *refs):
    if first:
        n2, g, w_up, b_up, w_down, ffn, dn2, g_down, g_up, g_bias, n2t = refs
    else:
        n2, g, w_up, b_up, w_down, d_in, u_in, b_in, ffn, dn2, g_down, g_up, g_bias, n2t = refs

    @pl.when(pl.program_id(0) == 0)
    def _():
        ffn[...] = jnp.zeros_like(ffn)
        dn2[...] = jnp.zeros_like(dn2)
        n2t[...] = n2[...].T

    pre_act = mm(n2[...], w_up[...], 1, 0) + b_up[...]
    value, slope = gelu_pair(pre_act)
    act = value.astype(bf16)
    ffn[...] += mm(act, w_down[...], 1, 0)
    d_pre = mm(g[...], w_down[...], 1, 1) * slope
    d_pre_b = d_pre.astype(bf16)
    dn2[...] += mm(d_pre_b, w_up[...], 1, 1)
    bias = jnp.sum(d_pre, 0, keepdims=True)
    down = mm(act, g[...], 0, 0)
    up = mm(n2t[...], d_pre_b, 1, 0)
    if first:
        g_down[...], g_up[...], g_bias[...] = down, up, bias
    else:
        g_down[...], g_up[...], g_bias[...] = d_in[...] + down, u_in[...] + up, b_in[...] + bias


def feed_forward(n2, g, w_up, b_up, w_down, before):
    tokens, width = n2.shape
    hidden = w_up.shape[1]
    block = min(512, hidden)
    full = pl.BlockSpec((tokens, width), lambda f: (0, 0))
    cols = pl.BlockSpec((width, block), lambda f: (0, f))
    line = pl.BlockSpec((1, block), lambda f: (0, f))
    rows = pl.BlockSpec((block, width), lambda f: (f, 0))
    extra = [] if before is None else list(before)
    return pl.pallas_call(
        functools.partial(feed_kernel, before is None),
        grid=(hidden // block,),
        in_specs=[full, full, cols, line, rows] + [rows, cols, line][: len(extra)],
        out_specs=[full, full, rows, cols, line],
        out_shape=[
            jax.ShapeDtypeStruct((tokens, width), f32),
            jax.ShapeDtypeStruct((tokens, width), f32),
            jax.ShapeDtypeStruct((hidden, width), f32),
            jax.ShapeDtypeStruct((width, hidden), f32),
            jax.ShapeDtypeStruct((1, hidden), f32),
        ],
        scratch_shapes=[pltpu.VMEM((width, tokens), bf16)],
        cost_estimate=pl.CostEstimate(
            flops=12 * tokens * width * hidden,
            bytes_accessed=(12 if before is None else 20) * width * hidden + 12 * tokens * width,
            transcendentals=tokens * hidden,
        ),
        compiler_params=pltpu.CompilerParams(vmem_limit_bytes=56 << 20),
        name="feed_forward",
    )(n2, g, w_up, b_up, w_down, *extra)


def proj_back_kernel(first, *refs):
    if first:
        n1, d_proj, w, part, grad, n1t = refs
    else:
        n1, d_proj, w, before, part, grad, n1t = refs

    @pl.when(pl.program_id(0) == 0)
    def _():
        part[...] = jnp.zeros_like(part)
        n1t[...] = n1[...].T

    part[...] += mm(d_proj[0], w[0], 1, 1)
    out = mm(n1t[...], d_proj[0], 1, 0)
    grad[0] = out if first else before[0] + out


def proj_back(n1, d_proj, w, before):
    tokens, width = n1.shape
    cols = d_proj.shape[2]
    full = pl.BlockSpec((tokens, width), lambda j: (0, 0))
    weight = pl.BlockSpec((1, width, cols), lambda j: (j, 0, 0))
    extra = [] if before is None else [before]
    return pl.pallas_call(
        functools.partial(proj_back_kernel, before is None),
        grid=(3,),
        in_specs=[full, pl.BlockSpec((1, tokens, cols), lambda j: (j, 0, 0)), weight] + [weight] * len(extra),
        out_specs=[full, weight],
        out_shape=[
            jax.ShapeDtypeStruct((tokens, width), f32),
            jax.ShapeDtypeStruct((3, width, cols), f32),
        ],
        scratch_shapes=[pltpu.VMEM((width, tokens), bf16)],
        cost_estimate=pl.CostEstimate(
            flops=12 * tokens * width * cols,
            bytes_accessed=30 * width * cols + 6 * tokens * width,
            transcendentals=0,
        ),
        name="proj_back",
    )(n1, d_proj, w, *extra)


def assemble_kernel(mask_ref, own_ref, other_ref, out_ref):
    half = pl.program_id(0)

    @pl.when(half == 0)
    def _():
        out_ref[...] = own_ref[...].astype(f32)

    @pl.when(half == 1)
    def _():
        out_ref[...] = other_ref[...].astype(f32)


def assemble(own, other, mask, blocks):
    width = own.shape[-1]
    rows = own.shape[0] // blocks
    own, other = own.reshape(blocks, rows, width), other.reshape(blocks, rows, width)
    return pl.pallas_call(
        assemble_kernel,
        grid_spec=pltpu.PrefetchScalarGridSpec(
            num_scalar_prefetch=1,
            grid=(2, blocks),
            in_specs=[
                pl.BlockSpec((1, rows, width), lambda h, i, m: (jnp.where(h == 0, i, blocks - 1), 0, 0)),
                pl.BlockSpec((1, rows, width), lambda h, i, m: (jnp.where(h == 0, 0, i), 0, 0)),
            ],
            out_specs=pl.BlockSpec((1, rows, width), lambda h, i, m: ((h * blocks + i) ^ m[0], 0, 0)),
        ),
        out_shape=jax.ShapeDtypeStruct((2 * blocks, rows, width), f32),
        cost_estimate=pl.CostEstimate(flops=0, bytes_accessed=12 * own.size, transcendentals=0),
        name="assemble",
    )(mask, own, other)


def swap(x, size):
    return lax.ppermute(x, "tensor", [(i, i ^ 1) for i in range(size)])


def after(x, *others):
    return lax.optimization_barrier((x, *others))[0]


def gather_cols(x, size, rank, got=None):
    if size != 2:
        return lax.all_gather(x, "tensor", axis=1, tiled=True)
    other = swap(x, size) if got is None else got
    return jnp.where(rank == 0, jnp.concatenate([x, other], 1), jnp.concatenate([other, x], 1))


def own_cols(x, size, rank):
    width = x.shape[1] // size
    return lax.dynamic_slice_in_dim(x, rank * width, width, 1)


def total_cols(part, size):
    if size != 2:
        return lax.psum(part, "tensor")
    return part + swap(part.astype(bf16), size).astype(f32)


def total_own_cols(part, size, rank):
    if size != 2:
        return lax.psum_scatter(part, "tensor", scatter_dimension=1, tiled=True)
    sent = own_cols(part, size, 1 - rank).astype(bf16)
    return own_cols(part, size, rank) + swap(sent, size).astype(f32)


def flip(x, bit, count):
    return lax.ppermute(x, "dp", [(i, i ^ (1 << bit)) for i in range(count)])


class DpSum:
    def __init__(self, grad, count, index):
        self.shape, self.count, self.index = grad.shape, count, index
        self.bits = count.bit_length() - 1
        self.kept = grad.reshape(-1, grad.shape[-1])
        self.at = 0
        self.send()

    def send(self):
        if self.at < self.bits:
            side = (self.index >> self.at) & 1
            half = self.kept.shape[0] // 2
            sent = lax.dynamic_slice_in_dim(self.kept, (1 - side) * half, half, 0).astype(bf16)
            self.mine = lax.dynamic_slice_in_dim(self.kept, side * half, half, 0)
            self.got = flip(sent, self.at, self.count)
        else:
            self.got = flip(self.kept, 2 * self.bits - 1 - self.at, self.count)

    def step(self):
        if self.at < self.bits:
            self.kept = self.mine + self.got.astype(f32)
            if self.at == self.bits - 1:
                self.kept = self.kept.astype(bf16)
        else:
            bit = 2 * self.bits - 1 - self.at
            pair = jnp.concatenate([self.kept, self.got], 0)
            if bit > 1:
                side = (self.index >> bit) & 1
                pair = jnp.where(side == 0, pair, jnp.concatenate([self.got, self.kept], 0))
            self.kept = pair
        self.at += 1
        self.send()

    def gather(self, *others):
        while self.at < 2 * self.bits - 1:
            if self.at == 2 * self.bits - 2:
                self.got = after(self.got, *others)
            self.step()
        mask = ((self.index & 1) << 1) | ((self.index >> 1) & 1)
        out = assemble(self.kept, self.got, mask.astype(jnp.int32).reshape(1), 2)
        return out.reshape(self.shape)


def tie(value, *sums):
    value, *got = lax.optimization_barrier((value, *[t.got for t in sums]))
    for t, x in zip(sums, got):
        t.got = x
    return value


def small_sum(x, count):
    if count & (count - 1):
        return lax.psum(x, "dp")
    for bit in range(count.bit_length() - 1):
        x = x + flip(x, bit, count)
    return x


def layer_norm(inputs, gain, shift):
    row_mean = jnp.mean(inputs, -1, keepdims=True)
    row_var = jnp.mean(inputs * inputs, -1, keepdims=True) - row_mean * row_mean
    inv_std = lax.rsqrt(row_var + norm_eps)
    centred = (inputs - row_mean) * inv_std
    return (centred * gain + shift, centred, inv_std)


def norm_back(upstream, centred, inv_std, gain):
    scaled = upstream * gain
    along = jnp.mean(scaled * centred, -1, keepdims=True)
    return inv_std * (scaled - jnp.mean(scaled, -1, keepdims=True) - centred * along)


def local(
    size,
    count,
    block_in,
    segment_ids,
    ln1_gain,
    ln1_bias,
    w_qkv,
    qv_bias,
    w_out,
    out_bias,
    ln2_gain,
    ln2_bias,
    w_up,
    up_bias,
    w_down,
    down_bias,
    cotangent,
):
    row_count, seq_len = segment_ids.shape
    token_count = block_in.shape[0]
    head_cols = w_qkv.shape[2]
    local_heads = head_cols // HEAD_DIM
    rank = lax.axis_index("tensor")
    index = lax.axis_index("dp")
    head_ids = rank * local_heads + jnp.arange(local_heads)
    slopes = jnp.exp2(-8.0 * (head_ids + 1).astype(f32) / HEADS)

    chunks = row_count if row_count == 2 else 1
    rows = row_count // chunks
    span = rows * seq_len

    def cut(x):
        return [x[c * span : (c + 1) * span] for c in range(chunks)]

    params = gather_cols(jnp.stack([ln1_gain, ln1_bias, ln2_gain, ln2_bias, out_bias]), size, rank)
    gain1, bias1, gain2, bias2, bias_out = params
    paired = size == 2 and chunks == 2
    qkv_bias = jnp.stack([qv_bias[0], jnp.zeros_like(qv_bias[0]), qv_bias[1]])[:, None, :]

    x_own = cut(block_in)
    g_own = cut(cotangent)
    seg = [segment_ids[c * rows : (c + 1) * rows] for c in range(chunks)]
    if paired:
        x_got = [swap(x_own[0], size)]
        x_got.append(swap(after(x_own[1], x_got[0]), size))
        x_all = [gather_cols(x, size, rank, got) for x, got in zip(x_own, x_got)]
        half = w_out.shape[0] // 2
        core = index & 1
        w_half = swap(after(lax.dynamic_slice_in_dim(w_out, core * half, half, 0), x_got[1]), size)
        w_rest = flip(w_half, 0, count)
        w_peer = jnp.where(core == 0, jnp.concatenate([w_half, w_rest], 0), jnp.concatenate([w_rest, w_half], 0))
        w_out_parts = [w_out, w_peer]
    else:
        x_all = [gather_cols(x, size, rank) for x in x_own]
        w_out_parts = [lax.all_gather(w_out, "tensor", axis=0, tiled=True)]
    st = []
    for c in range(chunks):
        inputs = x_all[c].astype(f32)
        norm1, centred1, inv1 = layer_norm(inputs, gain1, bias1)
        normed1 = norm1.astype(bf16)
        projected = (
            jnp.einsum("td,jde->jte", normed1, w_qkv, preferred_element_type=f32) + qkv_bias
        ).astype(bf16)
        context, lse = attend(projected, seg[c], slopes)
        if paired:
            context_parts = [context, swap(context, size)]
        else:
            context_parts = [lax.all_gather(context, "tensor", axis=1, tiled=True)]
        st.append(dict(inputs=inputs, normed1=normed1, projected=projected, context=context, lse=lse, parts=context_parts))
    if paired:
        g_got = [swap(after(g_own[0], st[0]["context"]), size)]
        g_got.append(swap(after(g_own[1], st[1]["context"]), size))
        g_all = [gather_cols(g, size, rank, got) for g, got in zip(g_own, g_got)]
    else:
        g_all = [gather_cols(g, size, rank) for g in g_own]
    grad_out, grad_qkv, ffn_grads = 0.0, None, None
    small = {}

    def tally(name, value):
        small[name] = small[name] + value if name in small else value

    outs = []
    for c in range(chunks):
        s = st[c]
        attn = sum(jnp.dot(a, w, preferred_element_type=f32) for a, w in zip(s["parts"], w_out_parts))
        resid = s["inputs"] + attn + bias_out
        norm2, centred2, inv2 = layer_norm(resid, gain2, bias2)
        normed2 = norm2.astype(bf16)
        ffn_part, norm2_part, *ffn_grads = feed_forward(normed2, g_all[c], w_up, up_bias[None], w_down, ffn_grads)
        if paired:
            s["part2"], s["got2"] = norm2_part, swap(norm2_part.astype(bf16), size)
        else:
            s["d_norm2"] = total_cols(norm2_part, size)
        tally("down", jnp.sum(g_own[c].astype(f32), 0))
        s.update(resid=resid, inv2=inv2, ffn_part=ffn_part)
    ffn_got = []
    down, up = DpSum(ffn_grads[0], count, index), DpSum(ffn_grads[1], count, index)
    small["up"] = ffn_grads[2][0]
    input_grads = []
    for c in range(chunks):
        s = st[c]
        if paired:
            got2 = s["got2"]
            if c > 0:
                got2 = tie(after(got2, st[0]["d_proj"]), down)
                down.step()
            d_norm2 = s["part2"] + got2.astype(f32)
        else:
            d_norm2 = s["d_norm2"]
        row_mean = jnp.mean(s["resid"], -1, keepdims=True)
        centred2 = (s["resid"] - row_mean) * s["inv2"]
        d_resid = g_all[c].astype(f32) + norm_back(d_norm2, centred2, s["inv2"], gain2)
        d_resid_b = d_resid.astype(bf16)
        if c == 0:
            d_resid_b = tie(d_resid_b, down, up)
            down.step()
            up.step()
        own_norm2 = own_cols(d_norm2, size, rank)
        tally("ln2_gain", jnp.sum(own_norm2 * own_cols(centred2, size, rank), 0))
        tally("ln2_bias", jnp.sum(own_norm2, 0))
        tally("out", jnp.sum(own_cols(d_resid, size, rank), 0))
        d_context = jnp.einsum("td,ed->te", d_resid_b, w_out, preferred_element_type=f32).astype(bf16)
        d_proj, sums = attend_back(s["projected"], s["context"], d_context, s["lse"], seg[c], slopes)
        tally("qv", jnp.sum(sums, 0))
        s["d_proj"] = d_proj
        if paired:
            sent = own_cols(s["ffn_part"], size, 1 - rank).astype(bf16)
            ffn_got.append(swap(after(sent, d_proj), size))
        if c > 0:
            d_proj = tie(d_proj, down, up)
            down.step()
            up.step()
        norm1_part, grad_qkv = proj_back(s["normed1"], d_proj, w_qkv, grad_qkv)
        row_mean1 = jnp.mean(s["inputs"], -1, keepdims=True)
        row_var1 = jnp.mean(s["inputs"] * s["inputs"], -1, keepdims=True) - row_mean1 * row_mean1
        inv1 = lax.rsqrt(row_var1 + norm_eps)
        centred1 = (s["inputs"] - row_mean1) * inv1
        scaled_part = norm1_part * gain1
        sums1 = jnp.stack([jnp.sum(scaled_part, -1), jnp.sum(scaled_part * centred1, -1)])
        if size == 2:
            sums1 = sums1 + swap(sums1, size)
        else:
            sums1 = lax.psum(sums1, "tensor")
        d_norm1 = total_own_cols(norm1_part, size, rank)
        own1 = own_cols(centred1, size, rank)
        means = sums1 / D
        back = inv1 * (d_norm1 * ln1_gain - means[0][:, None] - own1 * means[1][:, None])
        input_grads.append(own_cols(d_resid, size, rank) + back)
        tally("ln1_gain", jnp.sum(d_norm1 * own1, 0))
        tally("ln1_bias", jnp.sum(d_norm1, 0))
        grad_out = grad_out + mm(s["context"], d_resid_b, 0, 0)
    total_out, total_qkv = DpSum(grad_out, count, index), DpSum(grad_qkv, count, index)
    if paired:
        total_qkv.got, ffn_got[0], ffn_got[1] = lax.optimization_barrier((total_qkv.got, *ffn_got))
    for c in range(chunks):
        s = st[c]
        if paired:
            ffn = own_cols(s["ffn_part"], size, rank) + ffn_got[c].astype(f32)
        else:
            ffn = total_own_cols(s["ffn_part"], size, rank)
        outs.append((own_cols(s["resid"], size, rank) + ffn + down_bias).astype(bf16))
    names = ["ln1_gain", "ln1_bias", "qv", "out", "ln2_gain", "ln2_bias", "up", "down"]
    flat = jnp.concatenate([small[n].reshape(-1) for n in names])
    flat = small_sum(flat, count)
    grad_down, grad_up, grad_out = [t.gather() for t in (down, up, total_out)]
    grad_qkv = total_qkv.gather(flat, grad_down, grad_up)
    done, at = {}, 0
    for n in names:
        length = small[n].size
        done[n] = flat[at : at + length].reshape(small[n].shape)
        at += length
    return (
        jnp.concatenate(outs, 0),
        jnp.concatenate(input_grads, 0),
        done["ln1_gain"],
        done["ln1_bias"],
        grad_qkv,
        done["qv"],
        grad_out,
        done["out"],
        done["ln2_gain"],
        done["ln2_bias"],
        grad_up,
        done["up"],
        grad_down,
        done["down"],
    )


def solution(mesh):
    in_specs = (
        P("dp", "tensor"),
        P("dp", None),
        P("tensor"),
        P("tensor"),
        P(None, None, "tensor"),
        P(None, "tensor"),
        P("tensor", None),
        P("tensor"),
        P("tensor"),
        P("tensor"),
        P(None, "tensor"),
        P("tensor"),
        P("tensor", None),
        P("tensor"),
        P("dp", "tensor"),
    )
    out_specs = (
        P("dp", "tensor"),
        P("dp", "tensor"),
        P("tensor"),
        P("tensor"),
        P(None, None, "tensor"),
        P(None, "tensor"),
        P("tensor", None),
        P("tensor"),
        P("tensor"),
        P("tensor"),
        P(None, "tensor"),
        P("tensor"),
        P("tensor", None),
        P("tensor"),
    )
    body = functools.partial(local, mesh.shape["tensor"], mesh.shape["dp"])
    return jax.shard_map(body, mesh=mesh, in_specs=in_specs, out_specs=out_specs, check_vma=False)
```
